32 devices in a mesh: ctx: 16 (over z, y, core), tp: 2 (over x).
Axes of the slice: x: 2, y: 2, z: 4, core: 2. Of those that a mesh axis runs over, the one named last changes fastest.
Arguments:
- activations: bfloat16 [2048, 4096], P(('ctx', 'tp')), may hold values from -24 to 24
- query_weight: bfloat16 [4096, 4096], P(None, 'tp'), may hold values from -0.09375 to 0.09375
- key_weight: bfloat16 [4096, 1024], P(None, 'tp'), may hold values from -0.09375 to 0.09375
- value_weight: bfloat16 [4096, 1024], P(None, 'tp'), may hold values from -0.09375 to 0.09375
Outputs:
- attended: bfloat16 [2048, 4096], P('ctx', 'tp')
The draws below stay inside these ranges and needn't reach their ends.
All inputs are finite; a program needn't handle non-finite values.
Results may differ from the reference program's by a relative error of at most 0.012.
The reference program's roundings to bfloat16 on the way (of `queries`, `keys`, `values` and `weights`) count: a program that leaves them out, or rounds other values in their place, can miss the bound.
Values may be sent and summed in bfloat16 or wider, within the bound.
No kernel may reach another device: no remote copies, remote signals or barrier semaphores. Data moves between devices by JAX's collectives and lax.ppermute only.
A program may use at most 128 MiB of HBM per device.

```python
import math
import jax
import jax.numpy as jnp
from jax import lax

D = 4096
QH = 32
KVH = 8
HD = 128
S = 2048


def draw_activations(key, part):
    first_key = jax.random.fold_in(jax.random.fold_in(key, 11), 0)
    result = jax.random.normal(first_key, (S, D), jnp.float32)
    return jnp.clip(result, -6.0, 6.0).astype(jnp.bfloat16)


def block_scale(rng, dims, shards, low, largest):
    level = 1.0
    for position, blocks in shards:
        steps = jax.random.uniform(jax.random.fold_in(jax.random.fold_in(rng, 6), position), (blocks,), jnp.float32, low / len(shards), largest / len(shards))
        level = level * jnp.repeat(jnp.exp(steps), dims[position] // blocks).reshape((-1,) + (1,) * (len(dims) - 1 - position))
    return level


def noise(own_key, shape, scale, reach, shards=(), held_as=jnp.bfloat16):
    values = scale * jax.random.normal(own_key, shape, jnp.float32)
    if shards:
        values = values * block_scale(own_key, shape, shards, -0.22, 0.18)
    return jnp.clip(values, -reach, reach).astype(held_as)


def setup_inputs(seed: int = 0) -> dict:
    seeds = jax.random.split(jax.random.key(seed), 5)
    return {
        "activations": draw_activations(jax.random.fold_in(seeds[4], 71), 0),
        "query_weight": noise(seeds[1], (D, QH * HD), D ** -0.5, 0.09375, ((1, 2),)),
        "key_weight": noise(seeds[2], (D, KVH * HD), D ** -0.5, 0.09375, ((1, 2),)),
        "value_weight": noise(seeds[3], (D, KVH * HD), D ** -0.5, 0.09375, ((1, 2),)),
    }


THETA = 500000.0

def rotate(heads_in, positions):
    width = heads_in.shape[-1]
    half_width = width // 2
    frequency = THETA ** (-(jnp.arange(half_width).astype(jnp.float32) * 2.0 / width))
    angles = positions[:, None] * frequency[None, :]
    cosine = jnp.cos(angles)[:, None, :]
    sine_table = jnp.sin(angles)[:, None, :]
    front_half = heads_in[..., :half_width]
    back_half = heads_in[..., half_width:]
    return jnp.concatenate([front_half * cosine - back_half * sine_table, back_half * cosine + front_half * sine_table], axis=-1)

def reference(activations, query_weight, key_weight, value_weight):
    seq_len = activations.shape[0]
    positions = jnp.arange(seq_len).astype(jnp.float32)
    source = activations.astype(jnp.float32)
    queries = rotate(jnp.dot(source, query_weight.astype(jnp.float32), preferred_element_type=jnp.float32).reshape(seq_len, QH, HD), positions).astype(jnp.bfloat16)
    keys = rotate(jnp.dot(source, key_weight.astype(jnp.float32), preferred_element_type=jnp.float32).reshape(seq_len, KVH, HD), positions).astype(jnp.bfloat16)
    values = jnp.dot(source, value_weight.astype(jnp.float32), preferred_element_type=jnp.float32).astype(jnp.bfloat16).reshape(seq_len, KVH, HD)
    group = QH // KVH
    block = math.gcd(seq_len, 1024)
    count = seq_len // block
    scale = 1.0 / math.sqrt(HD)
    query_heads = jnp.transpose(queries, (1, 0, 2)).reshape(KVH, group, count, block, HD)
    key_heads = jnp.transpose(keys, (1, 0, 2))
    value_heads = jnp.transpose(values, (1, 0, 2))
    columns = jnp.arange(seq_len).astype(jnp.int32)

    def per_kv(items):
        query_group, key_head, value_head = items
        key_float = key_head.astype(jnp.float32)
        value_float = value_head.astype(jnp.float32)

        def per_block(inner):
            query_block, block_index = inner
            scores = jnp.dot(query_block.astype(jnp.float32), key_float.T, preferred_element_type=jnp.float32) * scale
            row_ids = (block_index * block + jnp.arange(block).astype(jnp.int32)).astype(jnp.int32)
            allowed = columns[None, :] <= row_ids[:, None]
            masked = jnp.where(allowed, scores, jnp.float32(-1e+30))
            row_top = lax.optimization_barrier(jnp.max(masked, axis=1))
            weights = jnp.where(allowed, jnp.exp(scores - row_top[:, None]), jnp.float32(0.0))
            totals = lax.optimization_barrier(jnp.sum(weights, axis=1))
            rounded = lax.optimization_barrier(weights.astype(jnp.bfloat16)).astype(jnp.float32)
            return jnp.dot(rounded, value_float, preferred_element_type=jnp.float32) / totals[:, None]

        def per_head(query_head):
            result = lax.map(per_block, (query_head, jnp.arange(count).astype(jnp.int32)))
            return result.reshape(seq_len, HD)
        return lax.map(per_head, query_group)
    outputs = lax.map(per_kv, (query_heads, key_heads, value_heads))
    outputs = jnp.transpose(outputs.reshape(QH, seq_len, HD), (1, 0, 2)).reshape(seq_len, QH * HD)
    return outputs.astype(jnp.bfloat16)
```

```python
import functools
import math

import jax
import jax.numpy as jnp
from jax import lax
from jax.experimental import pallas as pl
from jax.experimental.pallas import tpu as pltpu
from jax.sharding import PartitionSpec as P

HD = 128
THETA = 500000.0
NEGATIVE = -1e30
VMEM = pl.BlockSpec(memory_space=pltpu.VMEM)
LIMIT = 48 * 1024 * 1024


def tables(positions):
    frequency = THETA ** (-(jnp.arange(HD // 2).astype(jnp.float32) * 2.0 / HD))
    angles = positions.astype(jnp.float32)[:, None] * frequency[None, :]
    cosine, sine = jnp.cos(angles), jnp.sin(angles)
    return jnp.concatenate([cosine, cosine], axis=1), jnp.concatenate([-sine, sine], axis=1)


def turn(head, cosine, sine):
    return head * cosine + pltpu.roll(head, HD // 2, 1) * sine


def kv_kernel(parts, kv_heads, which_ref, *refs):
    rows_in = refs[:parts]
    key_w, value_w, cosine, sine, out_ref, total = refs[parts:]
    step = pl.program_id(0)
    depth = key_w.shape[0]
    rows = jnp.concatenate(
        [r[:, pl.ds(pl.multiple_of(step * depth, depth), depth)] for r in rows_in], axis=0
    )
    width = kv_heads * HD
    keys = jnp.dot(rows, key_w[...], preferred_element_type=jnp.float32)
    values = jnp.dot(rows, value_w[...], preferred_element_type=jnp.float32)

    @pl.when(step == 0)
    def _():
        total[:, :width] = keys
        total[:, width:] = values

    @pl.when(step > 0)
    def _():
        total[:, :width] += keys
        total[:, width:] += values

    @pl.when(step == pl.num_programs(0) - 1)
    def _():
        for h in range(kv_heads):
            cut = slice(h * HD, (h + 1) * HD)
            out_ref[:, cut] = turn(total[:, cut], cosine[...], sine[...]).astype(jnp.bfloat16)
        out_ref[:, width:] = total[:, width:].astype(jnp.bfloat16)


def project_kv(which, blocks, key_weight, value_weight, cosine, sine, kv_heads):
    rows = sum(b.shape[0] for b in blocks)
    model = key_weight.shape[0]
    width = kv_heads * HD
    depth = math.gcd(model, 1024)
    whole = lambda a: pl.BlockSpec(a.shape, lambda k, w: (0, 0))
    weight = pl.BlockSpec((depth, width), lambda k, w: (k, w[0]))
    return pl.pallas_call(
        functools.partial(kv_kernel, len(blocks), kv_heads),
        out_shape=jax.ShapeDtypeStruct((rows, 2 * width), jnp.bfloat16),
        grid_spec=pltpu.PrefetchScalarGridSpec(
            num_scalar_prefetch=1,
            grid=(model // depth,),
            in_specs=[whole(b) for b in blocks] + [weight, weight, whole(cosine), whole(sine)],
            out_specs=pl.BlockSpec((rows, 2 * width), lambda k, w: (0, 0)),
            scratch_shapes=[pltpu.VMEM((rows, 2 * width), jnp.float32)],
        ),
        compiler_params=pltpu.CompilerParams(vmem_limit_bytes=LIMIT),
        cost_estimate=pl.CostEstimate(
            flops=4 * rows * model * width, bytes_accessed=4 * model * width, transcendentals=0
        ),
    )(which, *blocks, key_weight, value_weight, cosine, sine)


def query_kernel(parts, which_ref, *refs):
    rows_in = refs[:parts]
    weight, cosine, sine, out_ref, gathered = refs[parts:]

    @pl.when(pl.program_id(0) == 0)
    def _():
        at = 0
        for r in rows_in:
            gathered[at : at + r.shape[0]] = r[...]
            at += r.shape[0]

    product = jnp.dot(gathered[...], weight[...], preferred_element_type=jnp.float32)
    for h in range(weight.shape[1] // HD):
        head = product[:, h * HD : (h + 1) * HD]
        out_ref[h] = turn(head, cosine[...], sine[...]).astype(jnp.bfloat16)


def project_q(which, blocks, query_weight, cosine, sine, heads):
    rows = sum(b.shape[0] for b in blocks)
    model = query_weight.shape[0]
    per_step = math.gcd(heads, 2)
    steps = heads // per_step
    whole = lambda a: pl.BlockSpec(a.shape, lambda k, w: (0, 0))
    return pl.pallas_call(
        functools.partial(query_kernel, len(blocks)),
        out_shape=jax.ShapeDtypeStruct((heads, rows, HD), jnp.bfloat16),
        grid_spec=pltpu.PrefetchScalarGridSpec(
            num_scalar_prefetch=1,
            grid=(steps,),
            in_specs=[whole(b) for b in blocks]
            + [
                pl.BlockSpec((model, per_step * HD), lambda n, w: (0, w[0] * steps + n)),
                whole(cosine),
                whole(sine),
            ],
            out_specs=pl.BlockSpec((per_step, rows, HD), lambda n, w: (n, 0, 0)),
            scratch_shapes=[pltpu.VMEM((rows, model), jnp.bfloat16)],
        ),
        compiler_params=pltpu.CompilerParams(vmem_limit_bytes=LIMIT),
        cost_estimate=pl.CostEstimate(
            flops=2 * rows * model * heads * HD, bytes_accessed=2 * model * heads * HD, transcendentals=0
        ),
    )(which, *blocks, query_weight, cosine, sine)


def attend_kernel(own_count, far_count, kv_heads, seen_ref, *refs):
    query_ref, query_pos, key_pos = refs[:3]
    own = refs[3 : 3 + own_count]
    far = refs[3 + own_count : 3 + own_count + far_count]
    out_ref = refs[3 + own_count + far_count]
    heads, rows, _ = query_ref.shape
    group = heads // kv_heads
    factor = math.log2(math.e) / math.sqrt(HD)
    allowed = key_pos[...] <= query_pos[...]
    hidden = [jnp.where(seen_ref[i] > 0, 0.0, -NEGATIVE) for i in range(far_count)]

    for kv_head in range(kv_heads):
        key_cut = slice(kv_head * HD, (kv_head + 1) * HD)
        value_cut = slice((kv_heads + kv_head) * HD, (kv_heads + kv_head + 1) * HD)

        @pl.loop(0, group)
        def _(member):
            head = kv_head * group + member
            query = query_ref[head]

            def score(block):
                return lax.dot_general(
                    query, block, (((1,), (1,)), ((), ())), preferred_element_type=jnp.float32
                )

            near = jnp.concatenate([score(r[:, key_cut]) for r in own], axis=1)
            near = jnp.where(allowed, near, NEGATIVE)
            top = jnp.max(near, axis=1, keepdims=True)
            distant = []
            for i, r in enumerate(far):
                scores = score(r[:, key_cut])
                distant.append(scores)
                top = jnp.maximum(top, jnp.max(scores, axis=1, keepdims=True) - hidden[i])
            limit = top * factor
            weights = jnp.exp2(near * factor - limit)
            total = jnp.sum(weights, axis=1, keepdims=True)
            weights = weights.astype(jnp.bfloat16)
            result = None
            at = 0
            for r in own:
                count = r.shape[0]
                term = jnp.dot(
                    weights[:, at : at + count], r[:, value_cut], preferred_element_type=jnp.float32
                )
                result = term if result is None else result + term
                at += count
            for i, r in enumerate(far):
                weights = jnp.exp2(distant[i] * factor - (limit + hidden[i]))
                total = total + jnp.sum(weights, axis=1, keepdims=True)
                result = result + jnp.dot(
                    weights.astype(jnp.bfloat16), r[:, value_cut], preferred_element_type=jnp.float32
                )
            out_ref[head] = (result / total).astype(jnp.bfloat16)


def attend(seen, queries, query_pos, key_pos, own, far, kv_heads):
    heads, rows, _ = queries.shape
    keys = sum(r.shape[0] for r in own) + sum(r.shape[0] for r in far)
    return pl.pallas_call(
        functools.partial(attend_kernel, len(own), len(far), kv_heads),
        out_shape=jax.ShapeDtypeStruct((heads, rows, HD), jnp.bfloat16),
        in_specs=[pl.BlockSpec(memory_space=pltpu.SMEM)] + [VMEM] * (3 + len(own) + len(far)),
        out_specs=VMEM,
        compiler_params=pltpu.CompilerParams(vmem_limit_bytes=LIMIT),
        cost_estimate=pl.CostEstimate(
            flops=4 * heads * rows * keys * HD,
            bytes_accessed=heads * rows * HD * 4,
            transcendentals=heads * rows * keys,
        ),
    )(seen, queries, query_pos, key_pos, *own, *far)


def local(activations, query_weight, key_weight, value_weight):
    tensor_count, context_count = lax.axis_size("tp"), lax.axis_size("ctx")
    tensor_index, context_index = lax.axis_index("tp"), lax.axis_index("ctx")
    rows_here = activations.shape[0]
    local_rows = rows_here * tensor_count
    heads_here = query_weight.shape[1] // HD
    kv_here = key_weight.shape[1] // HD
    pair = 2 if context_count % 2 == 0 and kv_here % 2 == 0 else 1
    kv_heads, heads = kv_here // pair, heads_here // pair
    places = context_count // pair
    inner = 2 ** (int(math.log2(places)) // 2) if places & (places - 1) == 0 else 1
    outer = places // inner
    half = context_index % pair
    place = context_index // pair
    far_out, far_in = place // inner, place % inner
    which = half.astype(jnp.int32)[None]

    def swap(block):
        return lax.ppermute(block, "ctx", [(i, i ^ 1) for i in range(context_count)])

    def device(o, i, c):
        return (o * inner + i) * pair + c

    blocks = [activations]
    owners = [tensor_index]
    for shift in range(1, tensor_count):
        blocks.append(
            lax.ppermute(activations, "tp", [(i, (i + shift) % tensor_count) for i in range(tensor_count)])
        )
        owners.append((tensor_index - shift) % tensor_count)
    held, starts = [], []
    for block, owner in zip(blocks, owners):
        for c in range(pair):
            held.append(block if c == 0 else swap(block))
            starts.append((place * pair + (half + c) % pair) * local_rows + owner * rows_here)
    positions = jnp.concatenate([s + jnp.arange(rows_here, dtype=jnp.int32) for s in starts])
    cosine, sine = tables(positions)

    own, far, seen = [], [], []
    piece = project_kv(which, held, key_weight, value_weight, cosine, sine, kv_heads)
    own.append(piece)
    columns = [piece]
    for hop in range(1, outer):
        links = [
            (device(o, i, c), device(o + hop, i, c))
            for o in range(outer - hop)
            for i in range(inner)
            for c in range(pair)
        ]
        columns.append(lax.ppermute(piece, "ctx", links))
        far.append(columns[-1])
        seen.append(far_out >= hop)
    for hop, column in enumerate(columns):
        for turn_by in range(1, inner):
            links = [
                (device(o, i, c), device(o, (i + turn_by) % inner, c))
                for o in range(hop, outer)
                for i in range(inner)
                for c in range(pair)
                if hop > 0 or i + turn_by < inner
            ]
            far.append(lax.ppermute(column, "ctx", links))
            seen.append((far_out >= hop) if hop > 0 else (far_in >= turn_by))
    queries = project_q(which, held, query_weight, cosine, sine, heads)
    seen = jnp.stack([s.astype(jnp.int32) for s in seen]) if seen else jnp.zeros((1,), jnp.int32)
    result = attend(seen, queries, positions[:, None], positions[None, :], own, far, kv_heads)

    result = result.reshape(heads, tensor_count, pair, rows_here, HD)
    result = jnp.transpose(result, (2, 1, 3, 0, 4))
    shift = jnp.stack(owners)
    result = jnp.zeros_like(result).at[:, shift].set(result) if tensor_count > 2 else (
        jnp.where(tensor_index == 0, result, result[:, ::-1]) if tensor_count == 2 else result
    )
    result = result.reshape(pair, local_rows, heads * HD)
    if pair == 1:
        return result[0]
    theirs = swap(result[1])
    first = jnp.where(half == 0, result[0], theirs)
    second = jnp.where(half == 0, theirs, result[0])
    return jnp.concatenate([first, second], axis=1)


def solution(mesh):
    in_specs = (P(("ctx", "tp"), None), P(None, "tp"), P(None, "tp"), P(None, "tp"))
    return jax.shard_map(local, mesh=mesh, in_specs=in_specs, out_specs=P("ctx", "tp"), check_vma=False)
```

```python
import functools
import math

import jax
import jax.numpy as jnp
from jax import lax
from jax.experimental import pallas as pl
from jax.experimental.pallas import tpu as pltpu
from jax.sharding import PartitionSpec as P

HD = 128
THETA = 500000.0
NEGATIVE = -1e30
HALF, OUTER, INNER, FACTS = 0, 1, 2, 3
VMEM = pl.BlockSpec(memory_space=pltpu.VMEM)


def tables(positions):
    frequency = THETA ** (-(jnp.arange(HD // 2).astype(jnp.float32) * 2.0 / HD))
    angles = positions.astype(jnp.float32)[:, None] * frequency[None, :]
    cosine, sine = jnp.cos(angles), jnp.sin(angles)
    return jnp.concatenate([cosine, cosine], axis=1), jnp.concatenate([-sine, sine], axis=1)


def turn(head, cosine, sine):
    return head * cosine + pltpu.roll(head, HD // 2, 1) * sine


def write_kv(product, cosine, sine, out_ref):
    width = product.shape[1] // 2
    for at in range(0, width, HD):
        cut = slice(at, at + HD)
        out_ref[:, cut] = turn(product[:, cut], cosine[...], sine[...]).astype(jnp.bfloat16)
    out_ref[:, width:] = product[:, width:].astype(jnp.bfloat16)


def first_kernel(parts, chunks, facts_ref, *refs):
    rows_in = refs[:parts]
    key_w, value_w, query_w, cosine, sine = refs[parts : parts + 5]
    out_ref, rows_ref, kv_ref, q_ref, kv_sem, q_sem, row_sem = refs[parts + 5 :]
    model = key_w.shape[0]
    depth = model // chunks
    width = kv_ref.shape[1] // 2
    wide = q_ref.shape[1]
    half = facts_ref[HALF]
    narrow_at = pl.multiple_of(half * width, width)
    wide_at = pl.multiple_of(half * wide, wide)
    count = rows_in[0].shape[0]
    own = pltpu.make_async_copy(rows_in[0], rows_ref.at[pl.ds(0, count)], row_sem)
    small, large = [], []
    for i in range(chunks):
        cut = pl.ds(i * depth, depth)
        for j, source in enumerate((key_w, value_w)):
            small.append(
                pltpu.make_async_copy(
                    source.at[cut, pl.ds(narrow_at, width)],
                    kv_ref.at[cut, pl.ds(j * width, width)],
                    kv_sem.at[i, j],
                )
            )
        large.append(
            pltpu.make_async_copy(
                query_w.at[cut, pl.ds(wide_at, wide)], q_ref.at[cut, :], q_sem.at[i]
            )
        )
    for copy in [own] + small + large:
        copy.start()
    for i in range(1, parts):
        rows_ref[i * count : (i + 1) * count, :] = rows_in[i][...]
    own.wait()
    product = None
    for i in range(chunks):
        small[2 * i].wait()
        small[2 * i + 1].wait()
        cut = slice(i * depth, (i + 1) * depth)
        term = jnp.dot(rows_ref[:, cut], kv_ref[cut, :], preferred_element_type=jnp.float32)
        product = term if product is None else product + term
    write_kv(product, cosine, sine, out_ref)
    for copy in large:
        copy.wait()


def later_kernel(parts, *refs):
    rows_in = refs[:parts]
    weight, cosine, sine, out_ref, rows_ref = refs[parts:]
    at = 0
    for r in rows_in:
        rows_ref[at : at + r.shape[0], :] = r[...]
        at += r.shape[0]
    product = jnp.dot(rows_ref[...], weight[...], preferred_element_type=jnp.float32)
    write_kv(product, cosine, sine, out_ref)


def query_kernel(parts, *refs):
    rows_in = refs[:parts]
    weight, cosine, sine, out_ref = refs[parts:]
    rows = jnp.concatenate([r[...] for r in rows_in], axis=0)
    heads = out_ref.shape[0]
    step = math.gcd(heads, 2)
    for at in range(0, heads, step):
        product = jnp.dot(
            rows, weight[:, at * HD : (at + step) * HD], preferred_element_type=jnp.float32
        )
        for h in range(step):
            head = product[:, h * HD : (h + 1) * HD]
            out_ref[at + h] = turn(head, cosine[...], sine[...]).astype(jnp.bfloat16)


SMEM = pl.BlockSpec(memory_space=pltpu.SMEM)
FAR = pl.BlockSpec(memory_space=pltpu.HBM)


def close(array):
    return pltpu.with_memory_space_constraint(array, pltpu.VMEM)


def params(megabytes):
    return pltpu.CompilerParams(vmem_limit_bytes=megabytes * 1024 * 1024)


def project_first(facts, blocks, key_weight, value_weight, query_weight, cosine, sine, kv_heads, heads):
    rows = sum(b.shape[0] for b in blocks)
    model = key_weight.shape[0]
    width = kv_heads * HD
    chunks = 4
    far = lambda a: pltpu.with_memory_space_constraint(a, pltpu.HBM)
    return pl.pallas_call(
        functools.partial(first_kernel, len(blocks), chunks),
        out_shape=[
            jax.ShapeDtypeStruct((rows, 2 * width), jnp.bfloat16),
            pltpu.VMEM((rows, model), jnp.bfloat16),
            pltpu.VMEM((model, 2 * width), jnp.bfloat16),
            pltpu.VMEM((model, heads * HD), jnp.bfloat16),
        ],
        in_specs=[SMEM, FAR] + [VMEM] * (len(blocks) - 1) + [FAR] * 3 + [VMEM] * 2,
        out_specs=[VMEM] * 4,
        scratch_shapes=[
            pltpu.SemaphoreType.DMA((chunks, 2)),
            pltpu.SemaphoreType.DMA((chunks,)),
            pltpu.SemaphoreType.DMA(()),
        ],
        compiler_params=params(24),
        cost_estimate=pl.CostEstimate(
            flops=4 * rows * model * width,
            bytes_accessed=2 * model * (heads * HD + 2 * width),
            transcendentals=0,
        ),
    )(facts, far(blocks[0]), *blocks[1:], far(key_weight), far(value_weight), far(query_weight), cosine, sine)


def project_later(blocks, weight, cosine, sine):
    rows = sum(b.shape[0] for b in blocks)
    return pl.pallas_call(
        functools.partial(later_kernel, len(blocks)),
        out_shape=[
            jax.ShapeDtypeStruct((rows, weight.shape[1]), jnp.bfloat16),
            pltpu.VMEM((rows, weight.shape[0]), jnp.bfloat16),
        ],
        in_specs=[VMEM] * (len(blocks) + 3),
        out_specs=[VMEM] * 2,
        compiler_params=params(24),
        cost_estimate=pl.CostEstimate(
            flops=2 * rows * weight.size, bytes_accessed=2 * weight.size, transcendentals=0
        ),
    )(*blocks, close(weight), cosine, sine)


def project_q(blocks, weight, cosine, sine, heads):
    rows = sum(b.shape[0] for b in blocks)
    return pl.pallas_call(
        functools.partial(query_kernel, len(blocks)),
        out_shape=jax.ShapeDtypeStruct((heads, rows, HD), jnp.bfloat16),
        in_specs=[VMEM] * (len(blocks) + 3),
        out_specs=VMEM,
        compiler_params=params(24),
        cost_estimate=pl.CostEstimate(
            flops=2 * rows * weight.size, bytes_accessed=2 * weight.size, transcendentals=0
        ),
    )(*[close(b) for b in blocks], close(weight), cosine, sine)


def attend_kernel(first, last, own_count, origins, kv_heads, pair, block_rows, facts_ref, *refs):
    refs = list(refs)
    query_ref = refs.pop(0)
    far_count = len(origins)
    own, far = refs[:own_count], refs[own_count : own_count + far_count]
    refs = refs[own_count + far_count :]
    if not first:
        top_in, total_in, sum_in = refs[:3]
        refs = refs[3:]
    heads, rows, _ = query_ref.shape
    group = heads // kv_heads
    factor = math.log2(math.e) / math.sqrt(HD)
    hidden = [
        jnp.where(facts_ref[OUTER if hop else INNER] >= (hop or turn_by), 0.0, -NEGATIVE)
        for hop, turn_by in origins
    ]
    blocks = rows // block_rows

    def position(index):
        result = facts_ref[FACTS + blocks] + index
        for i in range(1, blocks):
            start = facts_ref[FACTS + blocks + i] - i * block_rows
            result = jnp.where(index >= i * block_rows, start + index, result)
        return result

    if own_count:
        query_pos = position(lax.broadcasted_iota(jnp.int32, (rows, 1), 0))
        key_pos = position(lax.broadcasted_iota(jnp.int32, (1, rows), 1))

    def lane_max(block):
        if block.shape[1] % HD:
            return jnp.broadcast_to(jnp.max(block, axis=1, keepdims=True), (rows, HD))
        return functools.reduce(jnp.maximum, [block[:, i : i + HD] for i in range(0, block.shape[1], HD)])

    def lane_sum(block):
        if block.shape[1] % HD:
            whole = jnp.sum(block, axis=1, keepdims=True)
            return jnp.where(lax.broadcasted_iota(jnp.int32, (rows, HD), 1) == 0, whole, 0.0)
        return functools.reduce(jnp.add, [block[:, i : i + HD] for i in range(0, block.shape[1], HD)])

    for kv_head in range(kv_heads):
        key_cut = slice(kv_head * HD, (kv_head + 1) * HD)
        value_cut = slice((kv_heads + kv_head) * HD, (kv_heads + kv_head + 1) * HD)
        for member in range(group):
            head = kv_head * group + member
            query = query_ref[head]
            scores = []
            for r in own + far:
                scores.append(
                    lax.dot_general(
                        query, r[:, key_cut], (((1,), (1,)), ((), ())), preferred_element_type=jnp.float32
                    )
                )
            at = 0
            for i, r in enumerate(own):
                allowed = key_pos[:, at : at + r.shape[0]] <= query_pos
                scores[i] = jnp.where(allowed, scores[i], NEGATIVE)
                at += r.shape[0]
            bias = [0.0] * own_count + hidden
            top = None if first else top_in[head]
            for block, shift in zip(scores, bias):
                best = lane_max(block) - shift
                top = best if top is None else jnp.maximum(top, best)
            top = jnp.max(top, axis=1, keepdims=True)
            limit = top * factor
            if first:
                total = result = None
            else:
                before = jnp.exp2(top_in[head] * factor - limit)
                total = total_in[head] * before
                result = sum_in[head] * before
            for block, shift, r in zip(scores, bias, own + far):
                weights = jnp.exp2(block * factor - (limit + shift))
                part = lane_sum(weights)
                term = jnp.dot(
                    weights.astype(jnp.bfloat16), r[:, value_cut], preferred_element_type=jnp.float32
                )
                total = part if total is None else total + part
                result = term if result is None else result + term
            if not last:
                refs[0][head] = jnp.broadcast_to(top, (rows, HD))
                refs[1][head] = total
                refs[2][head] = result
            else:
                result = (result / jnp.sum(total, axis=1, keepdims=True)).astype(jnp.bfloat16)
                column = slice(head * HD, (head + 1) * HD)
                for i in range(blocks):
                    to = pl.multiple_of(facts_ref[FACTS + i] * block_rows, block_rows)
                    refs[i % pair][pl.ds(to, block_rows), column] = result[
                        i * block_rows : (i + 1) * block_rows
                    ]


def attend(facts, queries, own, far, origins, state, last, kv_heads, pair, block_rows):
    heads, rows, _ = queries.shape
    first = state is None
    keys = sum(r.shape[0] for r in own) + sum(r.shape[0] for r in far)
    held = jax.ShapeDtypeStruct((heads, rows, HD), jnp.float32)
    done = jax.ShapeDtypeStruct((rows // pair, heads * HD), jnp.bfloat16)
    operands = [queries] + list(own) + list(far) + ([] if first else list(state))
    return pl.pallas_call(
        functools.partial(attend_kernel, first, last, len(own), origins, kv_heads, pair, block_rows),
        out_shape=[done] * pair if last else [held] * 3,
        in_specs=[SMEM] + [VMEM] * len(operands),
        out_specs=[VMEM] * (pair if last else 3),
        compiler_params=params(24),
        cost_estimate=pl.CostEstimate(
            flops=4 * heads * rows * keys * HD,
            bytes_accessed=heads * rows * HD * 4,
            transcendentals=heads * rows * keys,
        ),
    )(facts, *operands)


def join_kernel(facts_ref, mine, theirs, out_ref):
    width = mine.shape[1]
    to = facts_ref[HALF] * width
    out_ref[:, pl.ds(pl.multiple_of(to, width), width)] = mine[...]
    out_ref[:, pl.ds(pl.multiple_of(width - to, width), width)] = theirs[...]


def local(activations, query_weight, key_weight, value_weight):
    tensor_count, context_count = lax.axis_size("tp"), lax.axis_size("ctx")
    tensor_index, context_index = lax.axis_index("tp"), lax.axis_index("ctx")
    rows_here = activations.shape[0]
    local_rows = rows_here * tensor_count
    heads_here = query_weight.shape[1] // HD
    kv_here = key_weight.shape[1] // HD
    pair = 2 if context_count % 2 == 0 and kv_here % 2 == 0 else 1
    kv_heads, heads = kv_here // pair, heads_here // pair
    places = context_count // pair
    inner = 2 ** (int(math.log2(places)) // 2) if places & (places - 1) == 0 else 1
    outer = places // inner
    half = context_index % pair
    place = context_index // pair
    far_out, far_in = place // inner, place % inner

    def swap(block):
        return lax.ppermute(block, "ctx", [(i, i ^ 1) for i in range(context_count)])

    def device(o, i, c):
        return (o * inner + i) * pair + c

    blocks, owners = [activations], [tensor_index]
    for shift in range(1, tensor_count):
        links = [(i, (i + shift) % tensor_count) for i in range(tensor_count)]
        blocks.append(lax.ppermute(activations, "tp", links))
        owners.append((tensor_index - shift) % tensor_count)
    owners = [owner for owner in owners for c in range(pair)]
    starts = [
        (place * pair + (half + i % pair) % pair) * local_rows + owner * rows_here
        for i, owner in enumerate(owners)
    ]
    facts = jnp.stack([half, far_out, far_in] + owners + starts).astype(jnp.int32)
    positions = jnp.concatenate([s + jnp.arange(rows_here, dtype=jnp.int32) for s in starts])
    cosine, sine = tables(positions)

    def after(value, others):
        return lax.optimization_barrier((value, list(others)))[0] if others else value

    def after(value, others):
        return lax.optimization_barrier((value, list(others)))[0] if others else value

    def both(wave):
        return [b if c == 0 else swap(b) for b in wave for c in range(pair)]

    hops = range(1, outer)

    def upward(piece):
        columns = {}
        for hop in hops:
            links = [
                (device(o, i, c), device(o + hop, i, c))
                for o in range(outer - hop)
                for i in range(inner)
                for c in range(pair)
            ]
            columns[hop] = lax.ppermute(piece, "ctx", links)
        return columns

    def aside(block, first, parts=(0,)):
        moved = []
        for turn_by in range(1, inner):
            links = [
                (device(o, i, c), device(o, (i + turn_by) % inner, c))
                for o in range(first, outer)
                for i in range(inner)
                for c in range(pair)
                if first > 0 or i + turn_by < inner
            ]
            block_in = lax.ppermute(block, "ctx", links)
            for part, hop in zip(jnp.split(block_in, len(parts)), parts):
                moved.append((part, (hop, turn_by)))
        return moved

    state = None

    def fold(own, pieces, last):
        nonlocal state
        limit = max(1, (1024 - local_rows) // max([block.shape[0] for block, _ in pieces] + [1]))
        for i in range(0, max(1, len(pieces)), limit):
            some = pieces[i : i + limit]
            state = attend(
                facts, queries, own if i == 0 else [], [block for block, _ in some], [o for _, o in some],
                state, last and i + limit >= len(pieces), kv_heads, pair, rows_here,
            )

    held = both(blocks[:1])
    count = len(held) * rows_here
    first, first_rows, kv_weight, q_weight = project_first(
        facts, held, key_weight, value_weight, query_weight, cosine[:count], sine[:count], kv_heads, heads
    )
    columns = upward(first)
    beside = aside(first, 0)
    early = [hop for hop in hops if hop != 2]
    gate = [columns[hop] for hop in early] + [b for b, _ in beside]
    late = both([after(b, gate) for b in blocks[1:]])
    second, second_rows = project_later(late, kv_weight, cosine[count:], sine[count:])
    pieces = [(columns[hop], (hop, 0)) for hop in hops] + beside
    if early:
        pieces += aside(jnp.concatenate([columns[hop] for hop in early], axis=0), 1, early)
    later = upward(second)
    more = [(later[hop], (hop, 0)) for hop in hops] + aside(second, 0)
    queries = project_q([first_rows, second_rows], q_weight, cosine, sine, heads)
    if early:
        block, parts = later[1], [1]
        if outer > 2:
            block, parts = jnp.concatenate([later[1], columns[2]], axis=0), [1, 2]
        more += aside(after(block, [queries]), 1, parts)
    fold([first, second], pieces, False)
    last = [m for hop in hops if hop > 1 for m in aside(after(later[hop], state[:1]), hop, [hop])]
    fold([], more, not last)
    if last:
        fold([], last, True)
    if pair == 1:
        return state[0]
    return pl.pallas_call(
        join_kernel,
        out_shape=jax.ShapeDtypeStruct((local_rows, pair * heads * HD), jnp.bfloat16),
        in_specs=[pl.BlockSpec(memory_space=pltpu.SMEM), VMEM, VMEM],
        out_specs=VMEM,
        compiler_params=params(4),
    )(facts, state[0], swap(state[1]))


def solution(mesh):
    in_specs = (P(("ctx", "tp"), None), P(None, "tp"), P(None, "tp"), P(None, "tp"))
    return jax.shard_map(local, mesh=mesh, in_specs=in_specs, out_specs=P("ctx", "tp"), check_vma=False)
```

```python
import functools
import math

import jax
import jax.numpy as jnp
from jax import lax
from jax.experimental import pallas as pl
from jax.experimental.pallas import tpu as pltpu
from jax.sharding import PartitionSpec as P

HD = 128
THETA = 500000.0
NEGATIVE = -1e30
HALF, OUTER, INNER, FACTS = 0, 1, 2, 3
VMEM = pl.BlockSpec(memory_space=pltpu.VMEM)


def tables(positions):
    frequency = THETA ** (-(jnp.arange(HD // 2).astype(jnp.float32) * 2.0 / HD))
    angles = positions.astype(jnp.float32)[:, None] * frequency[None, :]
    cosine, sine = jnp.cos(angles), jnp.sin(angles)
    return jnp.concatenate([cosine, cosine], axis=1), jnp.concatenate([-sine, sine], axis=1)


def turn(head, cosine, sine):
    return head * cosine + pltpu.roll(head, HD // 2, 1) * sine


def write_kv(product, cosine, sine, out_ref):
    width = product.shape[1] // 2
    for at in range(0, width, HD):
        cut = slice(at, at + HD)
        out_ref[:, cut] = turn(product[:, cut], cosine[...], sine[...]).astype(jnp.bfloat16)
    out_ref[:, width:] = product[:, width:].astype(jnp.bfloat16)


def load_kernel(chunks, facts_ref, *refs):
    rows_in, key_w, value_w, rows_ref, kv_ref, kv_sem, row_sem = refs
    depth = key_w.shape[0] // chunks
    width = kv_ref.shape[1] // 2
    at = pl.multiple_of(facts_ref[HALF] * width, width)
    copies = [pltpu.make_async_copy(rows_in, rows_ref, row_sem)]
    for i in range(chunks):
        cut = pl.ds(i * depth, depth)
        for j, source in enumerate((key_w, value_w)):
            copies.append(
                pltpu.make_async_copy(
                    source.at[cut, pl.ds(at, width)],
                    kv_ref.at[cut, pl.ds(j * width, width)],
                    kv_sem.at[i, j],
                )
            )
    for copy in copies:
        copy.start()
    for copy in copies:
        copy.wait()


def kv_kernel(parts, *refs):
    rows_in = refs[:parts]
    weight, cosine, sine, out_ref, rows_ref = refs[parts:]
    at = 0
    for r in rows_in:
        rows_ref[at : at + r.shape[0], :] = r[...]
        at += r.shape[0]
    product = jnp.dot(rows_ref[...], weight[...], preferred_element_type=jnp.float32)
    write_kv(product, cosine, sine, out_ref)


def query_kernel(parts, facts_ref, *refs):
    rows_in = refs[:parts]
    weight, cosine, sine, out_ref, rows_ref = refs[parts:]
    heads = out_ref.shape[0]
    at = 0
    for r in rows_in:
        rows_ref[at : at + r.shape[0], :] = r[...]
        at += r.shape[0]
    step = math.gcd(heads, 2)
    base = facts_ref[HALF] * (heads * HD)
    for at in range(0, heads, step):
        cut = pl.ds(pl.multiple_of(base + at * HD, step * HD), step * HD)
        product = jnp.dot(rows_ref[...], weight[:, cut], preferred_element_type=jnp.float32)
        for h in range(step):
            head = product[:, h * HD : (h + 1) * HD]
            out_ref[at + h] = turn(head, cosine[...], sine[...]).astype(jnp.bfloat16)


SMEM = pl.BlockSpec(memory_space=pltpu.SMEM)
FAR = pl.BlockSpec(memory_space=pltpu.HBM)


def close(array):
    return pltpu.with_memory_space_constraint(array, pltpu.VMEM)


def params(megabytes):
    return pltpu.CompilerParams(vmem_limit_bytes=megabytes * 1024 * 1024)


def far(array):
    return pltpu.with_memory_space_constraint(array, pltpu.HBM)


def load(facts, activations, key_weight, value_weight, width):
    model = key_weight.shape[0]
    chunks = 2
    return pl.pallas_call(
        functools.partial(load_kernel, chunks),
        out_shape=[
            pltpu.VMEM(activations.shape, jnp.bfloat16),
            pltpu.VMEM((model, 2 * width), jnp.bfloat16),
        ],
        in_specs=[SMEM] + [FAR] * 3,
        out_specs=[VMEM] * 2,
        scratch_shapes=[pltpu.SemaphoreType.DMA((chunks, 2)), pltpu.SemaphoreType.DMA(())],
        compiler_params=params(24),
        cost_estimate=pl.CostEstimate(flops=0, bytes_accessed=4 * model * width, transcendentals=0),
    )(facts, far(activations), far(key_weight), far(value_weight))


def project_kv(blocks, weight, cosine, sine):
    rows = sum(b.shape[0] for b in blocks)
    return pl.pallas_call(
        functools.partial(kv_kernel, len(blocks)),
        out_shape=[
            jax.ShapeDtypeStruct((rows, weight.shape[1]), jnp.bfloat16),
            pltpu.VMEM((rows, weight.shape[0]), jnp.bfloat16),
        ],
        in_specs=[VMEM] * (len(blocks) + 3),
        out_specs=[VMEM] * 2,
        compiler_params=params(24),
        cost_estimate=pl.CostEstimate(
            flops=2 * rows * weight.size, bytes_accessed=2 * weight.size, transcendentals=0
        ),
    )(*blocks, close(weight), cosine, sine)


def project_q(facts, blocks, weight, cosine, sine, heads):
    rows = sum(b.shape[0] for b in blocks)
    model = weight.shape[0]
    return pl.pallas_call(
        functools.partial(query_kernel, len(blocks)),
        out_shape=jax.ShapeDtypeStruct((heads, rows, HD), jnp.bfloat16),
        in_specs=[SMEM] + [VMEM] * len(blocks) + [VMEM] * 3,
        out_specs=VMEM,
        scratch_shapes=[
            pltpu.VMEM((rows, model), jnp.bfloat16),
        ],
        compiler_params=params(24),
        cost_estimate=pl.CostEstimate(
            flops=0, bytes_accessed=0, transcendentals=0
        ),
    )(facts, *[close(b) for b in blocks], close(weight), cosine, sine)


def attend_kernel(first, last, own_count, origins, kv_heads, pair, block_rows, facts_ref, *refs):
    refs = list(refs)
    query_ref = refs.pop(0)
    far_count = len(origins)
    own, far = refs[:own_count], refs[own_count : own_count + far_count]
    refs = refs[own_count + far_count :]
    if not first:
        top_in, total_in, sum_in = refs[:3]
        refs = refs[3:]
    heads, rows, _ = query_ref.shape
    group = heads // kv_heads
    factor = math.log2(math.e) / math.sqrt(HD)
    hidden = [
        jnp.where(facts_ref[OUTER if hop else INNER] >= (hop or turn_by), 0.0, -NEGATIVE)
        for hop, turn_by in origins
    ]
    blocks = rows // block_rows

    def position(index):
        result = facts_ref[FACTS + blocks] + index
        for i in range(1, blocks):
            start = facts_ref[FACTS + blocks + i] - i * block_rows
            result = jnp.where(index >= i * block_rows, start + index, result)
        return result

    if own_count:
        query_pos = position(lax.broadcasted_iota(jnp.int32, (rows, 1), 0))
        key_pos = position(lax.broadcasted_iota(jnp.int32, (1, rows), 1))

    def lane_max(block):
        if block.shape[1] % HD:
            return jnp.broadcast_to(jnp.max(block, axis=1, keepdims=True), (rows, HD))
        return functools.reduce(jnp.maximum, [block[:, i : i + HD] for i in range(0, block.shape[1], HD)])

    def lane_sum(block):
        if block.shape[1] % HD:
            whole = jnp.sum(block, axis=1, keepdims=True)
            return jnp.where(lax.broadcasted_iota(jnp.int32, (rows, HD), 1) == 0, whole, 0.0)
        return functools.reduce(jnp.add, [block[:, i : i + HD] for i in range(0, block.shape[1], HD)])

    for kv_head in range(kv_heads):
        key_cut = slice(kv_head * HD, (kv_head + 1) * HD)
        value_cut = slice((kv_heads + kv_head) * HD, (kv_heads + kv_head + 1) * HD)
        for member in range(group):
            head = kv_head * group + member
            query = query_ref[head]
            scores = []
            for r in own + far:
                scores.append(
                    lax.dot_general(
                        query, r[:, key_cut], (((1,), (1,)), ((), ())), preferred_element_type=jnp.float32
                    )
                )
            at = 0
            for i, r in enumerate(own):
                allowed = key_pos[:, at : at + r.shape[0]] <= query_pos
                scores[i] = jnp.where(allowed, scores[i], NEGATIVE)
                at += r.shape[0]
            bias = [0.0] * own_count + hidden
            top = None if first else top_in[head]
            for block, shift in zip(scores, bias):
                best = lane_max(block) - shift
                top = best if top is None else jnp.maximum(top, best)
            top = jnp.max(top, axis=1, keepdims=True)
            limit = top * factor
            if first:
                total = result = None
            else:
                before = jnp.exp2(top_in[head] * factor - limit)
                total = total_in[head] * before
                result = sum_in[head] * before
            for block, shift, r in zip(scores, bias, own + far):
                weights = jnp.exp2(block * factor - (limit + shift))
                part = lane_sum(weights)
                term = jnp.dot(
                    weights.astype(jnp.bfloat16), r[:, value_cut], preferred_element_type=jnp.float32
                )
                total = part if total is None else total + part
                result = term if result is None else result + term
            if not last:
                refs[0][head] = jnp.broadcast_to(top, (rows, HD))
                refs[1][head] = total
                refs[2][head] = result
            else:
                result = (result / jnp.sum(total, axis=1, keepdims=True)).astype(jnp.bfloat16)
                column = slice(head * HD, (head + 1) * HD)
                for i in range(blocks):
                    to = pl.multiple_of(facts_ref[FACTS + i] * block_rows, block_rows)
                    refs[i % pair][pl.ds(to, block_rows), column] = result[
                        i * block_rows : (i + 1) * block_rows
                    ]


def attend(facts, queries, own, far, origins, state, last, kv_heads, pair, block_rows):
    heads, rows, _ = queries.shape
    first = state is None
    keys = sum(r.shape[0] for r in own) + sum(r.shape[0] for r in far)
    held = jax.ShapeDtypeStruct((heads, rows, HD), jnp.float32)
    done = jax.ShapeDtypeStruct((rows // pair, heads * HD), jnp.bfloat16)
    operands = [queries] + list(own) + list(far) + ([] if first else list(state))
    return pl.pallas_call(
        functools.partial(attend_kernel, first, last, len(own), origins, kv_heads, pair, block_rows),
        out_shape=[done] * pair if last else [held] * 3,
        in_specs=[SMEM] + [VMEM] * len(operands),
        out_specs=[VMEM] * (pair if last else 3),
        compiler_params=params(24),
        cost_estimate=pl.CostEstimate(
            flops=4 * heads * rows * keys * HD,
            bytes_accessed=heads * rows * HD * 4,
            transcendentals=heads * rows * keys,
        ),
    )(facts, *operands)


def join_kernel(facts_ref, mine, theirs, out_ref):
    width = mine.shape[1]
    to = facts_ref[HALF] * width
    out_ref[:, pl.ds(pl.multiple_of(to, width), width)] = mine[...]
    out_ref[:, pl.ds(pl.multiple_of(width - to, width), width)] = theirs[...]


def local(activations, query_weight, key_weight, value_weight):
    tensor_count, context_count = lax.axis_size("tp"), lax.axis_size("ctx")
    tensor_index, context_index = lax.axis_index("tp"), lax.axis_index("ctx")
    rows_here = activations.shape[0]
    local_rows = rows_here * tensor_count
    heads_here = query_weight.shape[1] // HD
    kv_here = key_weight.shape[1] // HD
    pair = 2 if context_count % 2 == 0 and kv_here % 2 == 0 else 1
    kv_heads, heads = kv_here // pair, heads_here // pair
    places = context_count // pair
    inner = 2 ** (int(math.log2(places)) // 2) if places & (places - 1) == 0 else 1
    outer = places // inner
    half = context_index % pair
    place = context_index // pair
    far_out, far_in = place // inner, place % inner

    def swap(block):
        return lax.ppermute(block, "ctx", [(i, i ^ 1) for i in range(context_count)])

    def device(o, i, c):
        return (o * inner + i) * pair + c

    blocks, owners = [activations], [tensor_index]
    for shift in range(1, tensor_count):
        links = [(i, (i + shift) % tensor_count) for i in range(tensor_count)]
        blocks.append(lax.ppermute(activations, "tp", links))
        owners.append((tensor_index - shift) % tensor_count)
    owners = [owner for owner in owners for c in range(pair)]
    starts = [
        (place * pair + (half + i % pair) % pair) * local_rows + owner * rows_here
        for i, owner in enumerate(owners)
    ]
    facts = jnp.stack([half, far_out, far_in] + owners + starts).astype(jnp.int32)
    positions = jnp.concatenate([s + jnp.arange(rows_here, dtype=jnp.int32) for s in starts])
    cosine, sine = tables(positions)

    def after(value, others):
        return lax.optimization_barrier((value, list(others)))[0] if others else value

    def after(value, others):
        return lax.optimization_barrier((value, list(others)))[0] if others else value

    def both(wave):
        return [b if c == 0 else swap(b) for b in wave for c in range(pair)]

    hops = range(1, outer)

    def upward(piece, hop):
        links = [
            (device(o, i, c), device(o + hop, i, c))
            for o in range(outer - hop)
            for i in range(inner)
            for c in range(pair)
        ]
        return lax.ppermute(piece, "ctx", links)

    def aside(blocks, origins):
        moved = []
        for turn_by in range(1, inner):
            links = [
                (device(o, i, c), device(o, (i + turn_by) % inner, c))
                for o in range(outer)
                for i in range(inner)
                for c in range(pair)
                if any(o >= hop if hop else i + turn_by < inner for hop in origins)
            ]
            block = blocks[0] if len(blocks) == 1 else jnp.concatenate(blocks, axis=0)
            block = lax.ppermute(block, "ctx", links)
            at = 0
            for b, hop in zip(blocks, origins):
                moved.append((block[at : at + b.shape[0]], (hop, turn_by)))
                at += b.shape[0]
        return moved

    state = None

    def fold(own, pieces, last):
        nonlocal state
        limit = max(1, 1408 // max([block.shape[0] for block, _ in pieces] + [1]))
        for i in range(0, max(1, len(pieces)), limit):
            some = pieces[i : i + limit]
            state = attend(
                facts, queries, own if i == 0 else [], [block for block, _ in some], [o for _, o in some],
                state, last and i + limit >= len(pieces), kv_heads, pair, rows_here,
            )

    own_rows, kv_weight = load(facts, activations, key_weight, value_weight, kv_heads * HD)
    held = [own_rows] + both(blocks[:1])[1:]
    count = len(held) * rows_here
    first, first_rows = project_kv(held, kv_weight, cosine[:count], sine[:count])
    early = [hop for hop in hops if hop == 1]
    columns = {hop: upward(first, hop) for hop in early}
    beside = []
    gate = [columns[hop] for hop in early[:1]]
    late = both([after(b, gate) for b in blocks[1:]])
    second, second_rows = project_kv(late, kv_weight, cosine[count:], sine[count:])
    middle = []
    if early:
        chained = [columns[1]] if outer > 2 else []
        block = upward(jnp.concatenate(chained + [second], axis=0), 1)
        middle = [(block[first.shape[0] * len(chained) :], (1, 0))]
        if chained:
            middle.append((block[: first.shape[0]], (2, 0)))
    direct = []
    for hop in hops:
        if hop == 2:
            direct.append((upward(second, hop), (hop, 0)))
        elif hop > 2:
            both_waves = upward(jnp.concatenate([first, second], axis=0), hop)
            direct += [(both_waves[: first.shape[0]], (hop, 0)), (both_waves[first.shape[0] :], (hop, 0))]
    forwarded = aside([first] + [columns[hop] for hop in early[:1]] + [second], [0] + early[:1] + [0])
    queries = project_q(facts, [first_rows, second_rows], query_weight, cosine, sine, heads)
    again, last = [], []
    if middle:
        again = aside([after(b, [queries]) for b, _ in middle], [o[0] for _, o in middle])
    direct += [(columns[hop], (hop, 0)) for hop in early[1:]]
    if direct:
        last = aside([after(b, [m for m, _ in forwarded[:1]]) for b, _ in direct], [o[0] for _, o in direct])
    straight = [(columns[hop], (hop, 0)) for hop in early[:1]] + beside
    fold([first, second], straight + forwarded, False)
    fold([], middle + direct + again, not last)
    if last:
        fold([], last, True)
    if pair == 1:
        return state[0]
    return pl.pallas_call(
        join_kernel,
        out_shape=jax.ShapeDtypeStruct((local_rows, pair * heads * HD), jnp.bfloat16),
        in_specs=[pl.BlockSpec(memory_space=pltpu.SMEM), VMEM, VMEM],
        out_specs=VMEM,
        compiler_params=params(4),
    )(facts, state[0], swap(state[1]))


def solution(mesh):
    in_specs = (P(("ctx", "tp"), None), P(None, "tp"), P(None, "tp"), P(None, "tp"))
    return jax.shard_map(local, mesh=mesh, in_specs=in_specs, out_specs=P("ctx", "tp"), check_vma=False)
```

```python
import functools
import math

import jax
import jax.numpy as jnp
from jax import lax
from jax.experimental import pallas as pl
from jax.experimental.pallas import tpu as pltpu
from jax.sharding import PartitionSpec as P

HD = 128
THETA = 500000.0
NEGATIVE = -1e30
HALF, OUTER, INNER, FACTS = 0, 1, 2, 3
VMEM = pl.BlockSpec(memory_space=pltpu.VMEM)


def tables(positions):
    frequency = THETA ** (-(jnp.arange(HD // 2).astype(jnp.float32) * 2.0 / HD))
    angles = positions.astype(jnp.float32)[:, None] * frequency[None, :]
    cosine, sine = jnp.cos(angles), jnp.sin(angles)
    return jnp.concatenate([cosine, cosine], axis=1), jnp.concatenate([-sine, sine], axis=1)


def turn(head, cosine, sine):
    return head * cosine + pltpu.roll(head, HD // 2, 1) * sine


def write_kv(product, cosine, sine, out_ref):
    width = product.shape[1] // 2
    for at in range(0, width, HD):
        cut = slice(at, at + HD)
        out_ref[:, cut] = turn(product[:, cut], cosine[...], sine[...]).astype(jnp.bfloat16)
    out_ref[:, width:] = product[:, width:].astype(jnp.bfloat16)


def load_kernel(chunks, facts_ref, *refs):
    rows_in, key_w, value_w, rows_ref, kv_ref, kv_sem, row_sem = refs
    depth = key_w.shape[0] // chunks
    width = kv_ref.shape[1] // 2
    at = pl.multiple_of(facts_ref[HALF] * width, width)
    copies = [pltpu.make_async_copy(rows_in, rows_ref, row_sem)]
    for i in range(chunks):
        cut = pl.ds(i * depth, depth)
        for j, source in enumerate((key_w, value_w)):
            copies.append(
                pltpu.make_async_copy(
                    source.at[cut, pl.ds(at, width)],
                    kv_ref.at[cut, pl.ds(j * width, width)],
                    kv_sem.at[i, j],
                )
            )
    for copy in copies:
        copy.start()
    for copy in copies:
        copy.wait()


def kv_kernel(parts, *refs):
    rows_in = refs[:parts]
    weight, cosine, sine, out_ref, rows_ref = refs[parts:]
    at = 0
    for r in rows_in:
        rows_ref[at : at + r.shape[0], :] = r[...]
        at += r.shape[0]
    product = jnp.dot(rows_ref[...], weight[...], preferred_element_type=jnp.float32)
    write_kv(product, cosine, sine, out_ref)


def query_kernel(parts, facts_ref, *refs):
    rows_in = refs[:parts]
    weight, cosine, sine, out_ref, rows_ref = refs[parts:]
    heads = out_ref.shape[0]
    at = 0
    for r in rows_in:
        rows_ref[at : at + r.shape[0], :] = r[...]
        at += r.shape[0]
    step = math.gcd(heads, 2)
    base = facts_ref[HALF] * (heads * HD)
    for at in range(0, heads, step):
        cut = pl.ds(pl.multiple_of(base + at * HD, step * HD), step * HD)
        product = jnp.dot(rows_ref[...], weight[:, cut], preferred_element_type=jnp.float32)
        for h in range(step):
            head = product[:, h * HD : (h + 1) * HD]
            out_ref[at + h] = turn(head, cosine[...], sine[...]).astype(jnp.bfloat16)


SMEM = pl.BlockSpec(memory_space=pltpu.SMEM)
FAR = pl.BlockSpec(memory_space=pltpu.HBM)


def close(array):
    return pltpu.with_memory_space_constraint(array, pltpu.VMEM)


def params(megabytes):
    return pltpu.CompilerParams(vmem_limit_bytes=megabytes * 1024 * 1024)


def far(array):
    return pltpu.with_memory_space_constraint(array, pltpu.HBM)


def load(facts, activations, key_weight, value_weight, width):
    model = key_weight.shape[0]
    chunks = 2
    return pl.pallas_call(
        functools.partial(load_kernel, chunks),
        out_shape=[
            pltpu.VMEM(activations.shape, jnp.bfloat16),
            pltpu.VMEM((model, 2 * width), jnp.bfloat16),
        ],
        in_specs=[SMEM] + [FAR] * 3,
        out_specs=[VMEM] * 2,
        scratch_shapes=[pltpu.SemaphoreType.DMA((chunks, 2)), pltpu.SemaphoreType.DMA(())],
        compiler_params=params(24),
        cost_estimate=pl.CostEstimate(flops=0, bytes_accessed=4 * model * width, transcendentals=0),
    )(facts, far(activations), far(key_weight), far(value_weight))


def project_kv(blocks, weight, cosine, sine):
    rows = sum(b.shape[0] for b in blocks)
    return pl.pallas_call(
        functools.partial(kv_kernel, len(blocks)),
        out_shape=[
            jax.ShapeDtypeStruct((rows, weight.shape[1]), jnp.bfloat16),
            pltpu.VMEM((rows, weight.shape[0]), jnp.bfloat16),
        ],
        in_specs=[VMEM] * (len(blocks) + 3),
        out_specs=[VMEM] * 2,
        compiler_params=params(24),
        cost_estimate=pl.CostEstimate(
            flops=2 * rows * weight.size, bytes_accessed=2 * weight.size, transcendentals=0
        ),
    )(*blocks, close(weight), cosine, sine)


def project_q(facts, blocks, weight, cosine, sine, heads):
    rows = sum(b.shape[0] for b in blocks)
    model = weight.shape[0]
    return pl.pallas_call(
        functools.partial(query_kernel, len(blocks)),
        out_shape=jax.ShapeDtypeStruct((heads, rows, HD), jnp.bfloat16),
        in_specs=[SMEM] + [VMEM] * len(blocks) + [VMEM] * 3,
        out_specs=VMEM,
        scratch_shapes=[
            pltpu.VMEM((rows, model), jnp.bfloat16),
        ],
        compiler_params=params(24),
        cost_estimate=pl.CostEstimate(
            flops=0, bytes_accessed=0, transcendentals=0
        ),
    )(facts, *[close(b) for b in blocks], close(weight), cosine, sine)


def attend_kernel(first, last, own_count, origins, kv_heads, pair, block_rows, facts_ref, *refs):
    refs = list(refs)
    query_ref = refs.pop(0)
    far_count = len(origins)
    own, far = refs[:own_count], refs[own_count : own_count + far_count]
    refs = refs[own_count + far_count :]
    if not first:
        top_in, total_in, sum_in = refs[:3]
        refs = refs[3:]
    heads, rows, _ = query_ref.shape
    group = heads // kv_heads
    factor = math.log2(math.e) / math.sqrt(HD)
    hidden = [
        jnp.where(facts_ref[OUTER if hop else INNER] >= (hop or turn_by), 0.0, -NEGATIVE)
        for hop, turn_by in origins
    ]
    blocks = rows // block_rows

    def position(index):
        result = facts_ref[FACTS + blocks] + index
        for i in range(1, blocks):
            start = facts_ref[FACTS + blocks + i] - i * block_rows
            result = jnp.where(index >= i * block_rows, start + index, result)
        return result

    if own_count:
        query_pos = position(lax.broadcasted_iota(jnp.int32, (rows, 1), 0))
        key_pos = position(lax.broadcasted_iota(jnp.int32, (1, rows), 1))

    def lane_max(block):
        if block.shape[1] % HD:
            return jnp.broadcast_to(jnp.max(block, axis=1, keepdims=True), (rows, HD))
        return functools.reduce(jnp.maximum, [block[:, i : i + HD] for i in range(0, block.shape[1], HD)])

    def lane_sum(block):
        if block.shape[1] % HD:
            whole = jnp.sum(block, axis=1, keepdims=True)
            return jnp.where(lax.broadcasted_iota(jnp.int32, (rows, HD), 1) == 0, whole, 0.0)
        return functools.reduce(jnp.add, [block[:, i : i + HD] for i in range(0, block.shape[1], HD)])

    for kv_head in range(kv_heads):
        key_cut = slice(kv_head * HD, (kv_head + 1) * HD)
        value_cut = slice((kv_heads + kv_head) * HD, (kv_heads + kv_head + 1) * HD)
        for member in range(group):
            head = kv_head * group + member
            query = query_ref[head]
            scores = []
            for r in own + far:
                scores.append(
                    lax.dot_general(
                        query, r[:, key_cut], (((1,), (1,)), ((), ())), preferred_element_type=jnp.float32
                    )
                )
            at = 0
            for i, r in enumerate(own):
                allowed = key_pos[:, at : at + r.shape[0]] <= query_pos
                scores[i] = jnp.where(allowed, scores[i], NEGATIVE)
                at += r.shape[0]
            bias = [0.0] * own_count + hidden
            top = None if first else top_in[head]
            for block, shift in zip(scores, bias):
                best = lane_max(block) - shift
                top = best if top is None else jnp.maximum(top, best)
            top = jnp.max(top, axis=1, keepdims=True)
            limit = top * factor
            if first:
                total = result = None
            else:
                before = jnp.exp2(top_in[head] * factor - limit)
                total = total_in[head] * before
                result = sum_in[head] * before
            for block, shift, r in zip(scores, bias, own + far):
                weights = jnp.exp2(block * factor - (limit + shift))
                part = lane_sum(weights)
                term = jnp.dot(
                    weights.astype(jnp.bfloat16), r[:, value_cut], preferred_element_type=jnp.float32
                )
                total = part if total is None else total + part
                result = term if result is None else result + term
            if not last:
                refs[0][head] = jnp.broadcast_to(top, (rows, HD))
                refs[1][head] = total
                refs[2][head] = result
            else:
                result = (result / jnp.sum(total, axis=1, keepdims=True)).astype(jnp.bfloat16)
                column = slice(head * HD, (head + 1) * HD)
                for i in range(blocks):
                    to = pl.multiple_of(facts_ref[FACTS + i] * block_rows, block_rows)
                    refs[i % pair][pl.ds(to, block_rows), column] = result[
                        i * block_rows : (i + 1) * block_rows
                    ]


def attend(facts, queries, own, far, origins, state, last, kv_heads, pair, block_rows):
    heads, rows, _ = queries.shape
    first = state is None
    keys = sum(r.shape[0] for r in own) + sum(r.shape[0] for r in far)
    held = jax.ShapeDtypeStruct((heads, rows, HD), jnp.float32)
    done = jax.ShapeDtypeStruct((rows // pair, heads * HD), jnp.bfloat16)
    operands = [queries] + list(own) + list(far) + ([] if first else list(state))
    return pl.pallas_call(
        functools.partial(attend_kernel, first, last, len(own), origins, kv_heads, pair, block_rows),
        out_shape=[done] * pair if last else [held] * 3,
        in_specs=[SMEM] + [VMEM] * len(operands),
        out_specs=[VMEM] * (pair if last else 3),
        compiler_params=params(24),
        cost_estimate=pl.CostEstimate(
            flops=4 * heads * rows * keys * HD,
            bytes_accessed=heads * rows * HD * 4,
            transcendentals=heads * rows * keys,
        ),
    )(facts, *operands)


def join_kernel(facts_ref, mine, theirs, out_ref):
    width = mine.shape[1]
    to = facts_ref[HALF] * width
    out_ref[:, pl.ds(pl.multiple_of(to, width), width)] = mine[...]
    out_ref[:, pl.ds(pl.multiple_of(width - to, width), width)] = theirs[...]


def local(activations, query_weight, key_weight, value_weight):
    tensor_count, context_count = lax.axis_size("tp"), lax.axis_size("ctx")
    tensor_index, context_index = lax.axis_index("tp"), lax.axis_index("ctx")
    rows_here = activations.shape[0]
    local_rows = rows_here * tensor_count
    heads_here = query_weight.shape[1] // HD
    kv_here = key_weight.shape[1] // HD
    pair = 2 if context_count % 2 == 0 and kv_here % 2 == 0 else 1
    kv_heads, heads = kv_here // pair, heads_here // pair
    places = context_count // pair
    inner = 2 ** (int(math.log2(places)) // 2) if places & (places - 1) == 0 else 1
    outer = places // inner
    half = context_index % pair
    place = context_index // pair
    far_out, far_in = place // inner, place % inner

    def swap(block):
        return lax.ppermute(block, "ctx", [(i, i ^ 1) for i in range(context_count)])

    def device(o, i, c):
        return (o * inner + i) * pair + c

    blocks, owners = [activations], [tensor_index]
    for shift in range(1, tensor_count):
        links = [(i, (i + shift) % tensor_count) for i in range(tensor_count)]
        blocks.append(lax.ppermute(activations, "tp", links))
        owners.append((tensor_index - shift) % tensor_count)
    owners = [owner for owner in owners for c in range(pair)]
    starts = [
        (place * pair + (half + i % pair) % pair) * local_rows + owner * rows_here
        for i, owner in enumerate(owners)
    ]
    facts = jnp.stack([half, far_out, far_in] + owners + starts).astype(jnp.int32)
    positions = jnp.concatenate([s + jnp.arange(rows_here, dtype=jnp.int32) for s in starts])
    cosine, sine = tables(positions)

    def after(value, others):
        return lax.optimization_barrier((value, list(others)))[0] if others else value

    def after(value, others):
        return lax.optimization_barrier((value, list(others)))[0] if others else value

    def both(wave):
        return [b if c == 0 else swap(b) for b in wave for c in range(pair)]

    hops = range(1, outer)

    def upward(piece, hop):
        links = [
            (device(o, i, c), device(o + hop, i, c))
            for o in range(outer - hop)
            for i in range(inner)
            for c in range(pair)
        ]
        return lax.ppermute(piece, "ctx", links)

    def aside(blocks, origins):
        moved = []
        for turn_by in range(1, inner):
            links = [
                (device(o, i, c), device(o, (i + turn_by) % inner, c))
                for o in range(outer)
                for i in range(inner)
                for c in range(pair)
                if any(o >= hop if hop else i + turn_by < inner for hop in origins)
            ]
            block = blocks[0] if len(blocks) == 1 else jnp.concatenate(blocks, axis=0)
            block = lax.ppermute(block, "ctx", links)
            at = 0
            for b, hop in zip(blocks, origins):
                moved.append((block[at : at + b.shape[0]], (hop, turn_by)))
                at += b.shape[0]
        return moved

    state = None

    def fold(own, pieces, last):
        nonlocal state
        limit = max(1, 1408 // max([block.shape[0] for block, _ in pieces] + [1]))
        for i in range(0, max(1, len(pieces)), limit):
            some = pieces[i : i + limit]
            state = attend(
                facts, queries, own if i == 0 else [], [block for block, _ in some], [o for _, o in some],
                state, last and i + limit >= len(pieces), kv_heads, pair, rows_here,
            )

    own_rows, kv_weight = load(facts, activations, key_weight, value_weight, kv_heads * HD)
    held = [own_rows] + both(blocks[:1])[1:]
    count = len(held) * rows_here
    first, first_rows = project_kv(held, kv_weight, cosine[:count], sine[:count])
    early = [hop for hop in hops if hop == 1]
    columns = {hop: upward(first, hop) for hop in early}
    beside = []
    gate = [columns[hop] for hop in early[:1]]
    late = both([after(b, gate) for b in blocks[1:]])
    second, second_rows = project_kv(late, kv_weight, cosine[count:], sine[count:])
    middle = []
    if early:
        chained = [columns[1]] if outer > 2 else []
        block = upward(jnp.concatenate(chained + [second], axis=0), 1)
        middle = [(block[first.shape[0] * len(chained) :], (1, 0))]
        if chained:
            middle.append((block[: first.shape[0]], (2, 0)))
    direct = []
    for hop in hops:
        if hop == 2:
            direct.append((upward(second, hop), (hop, 0)))
        elif hop > 2:
            both_waves = upward(jnp.concatenate([first, second], axis=0), hop)
            direct += [(both_waves[: first.shape[0]], (hop, 0)), (both_waves[first.shape[0] :], (hop, 0))]
    forwarded = aside([first] + [columns[hop] for hop in early[:1]] + [second], [0] + early[:1] + [0])
    queries = project_q(facts, [first_rows, second_rows], query_weight, cosine, sine, heads)
    straight = [(columns[hop], (hop, 0)) for hop in early]
    fold([first, second], straight, not middle)
    again, last = [], []
    if middle:
        again = aside([after(b, state[:1]) for b, _ in middle], [o[0] for _, o in middle])
    if direct:
        last = aside([after(b, [m for m, _ in forwarded[:1]]) for b, _ in direct], [o[0] for _, o in direct])
    if middle:
        fold([], forwarded + middle + direct + again, not last)
    if last:
        fold([], last, True)
    if pair == 1:
        return state[0]
    return pl.pallas_call(
        join_kernel,
        out_shape=jax.ShapeDtypeStruct((local_rows, pair * heads * HD), jnp.bfloat16),
        in_specs=[pl.BlockSpec(memory_space=pltpu.SMEM), VMEM, VMEM],
        out_specs=VMEM,
        compiler_params=params(4),
    )(facts, state[0], swap(state[1]))


def solution(mesh):
    in_specs = (P(("ctx", "tp"), None), P(None, "tp"), P(None, "tp"), P(None, "tp"))
    return jax.shard_map(local, mesh=mesh, in_specs=in_specs, out_specs=P("ctx", "tp"), check_vma=False)
```
